256 devices in a mesh: row: 16 (over z_lo, x), col: 16 (over y, z_hi, core).
Axes of the slice: x: 4, y: 4, z: 8 (z_hi: 2, z_lo: 4; z = z_hi * 4 + z_lo), core: 2. Of those that a mesh axis runs over, the one named last changes fastest.
Arguments:
- homolog_matrix: bfloat16 [128, 1280, 64], P('row', 'col'), may hold values from -6 to 6
- contact_matrix: bfloat16 [1280, 1280, 128], P('row', 'col'), may hold values from -24 to 24
- genuine_homolog_total: int32 [1], replicated, may hold values from 1 to 128
- genuine_chain_length: int32 [1], replicated, may hold values from 640 to 1280
- tensor_product_matrices: bfloat16 [1, 64, 64], replicated, may hold values from -0.75 to 0.75
- tensor_product_final: bfloat16 [1, 1024, 128], replicated, may hold values from -0.75 to 0.75
- mixing_value_gate_matrix: bfloat16 [1, 64, 512], replicated, may hold values from -0.75 to 0.75
- mixing_logit_matrix: bfloat16 [1, 128, 8], replicated
- mixing_final_matrix: bfloat16 [1, 256, 64], replicated, may hold values from -1.5 to 1.5
- feedforward_gate_expand: bfloat16 [1, 128, 1024], replicated, may hold values from -0.5 to 0.5
- feedforward_shrink_matrix: bfloat16 [1, 512, 128], replicated, may hold values from -0.25 to 0.25
Outputs:
- msa_out: bfloat16 [128, 1280, 64], P('row', 'col')
- pair_out: bfloat16 [1280, 1280, 128], P('row', 'col')
The draws below stay inside these ranges and needn't reach their ends.
Inputs may be any that keep to these rules, and one draw needn't show every extreme that they name: Sequences from genuine_homolog_total on are padding. Residues from genuine_chain_length on are padding.
All inputs are finite; a program needn't handle non-finite values.
Results may differ from the reference program's by a relative error of at most 0.0065.
The reference program's roundings to bfloat16 on the way count: a program that leaves them out, or rounds other values in their place, can miss the bound.
Values may be sent and summed in bfloat16 or wider, within the bound.
No kernel may reach another device: no remote copies, remote signals or barrier semaphores. Data moves between devices by JAX's collectives and lax.ppermute only.
A program may use at most 64 MiB of HBM per device.

```python
import math
import jax
import jax.numpy as jnp
from jax import lax

ALIGNED_FEATURES = 64
C_Z = 128
PRODUCT_FEATURES = 32
ATTENTION_GROUPS = 8
GROUP_FEATURES = 32
TRANS = 512
MODULE_REPEATS = 1
HOMOLOG_TOTAL = 128
CHAIN_LENGTH = 1280


def pair_law(key):
    base = jax.random.fold_in(key, 7011)
    key_dirs = jax.random.fold_in(base, 0)
    key_field = jax.random.fold_in(base, 1)
    key_rows = jax.random.fold_in(base, 3)
    key_noise = jax.random.fold_in(base, 4)
    key_rest = jax.random.fold_in(base, 6)
    raw = jax.random.normal(key_dirs, (MODULE_REPEATS, C_Z, ATTENTION_GROUPS), jnp.float32)
    raw = raw - jnp.mean(raw, axis=1, keepdims=True)
    basis = jnp.linalg.qr(raw.transpose(1, 0, 2).reshape(C_Z, MODULE_REPEATS * ATTENTION_GROUPS))[0]
    directions = basis.reshape(C_Z, MODULE_REPEATS, ATTENTION_GROUPS).transpose(1, 0, 2) * math.sqrt(C_Z)
    rest = jax.random.normal(key_rest, (MODULE_REPEATS, C_Z, ATTENTION_GROUPS), jnp.float32) * (2.0 / math.sqrt(C_Z))
    field = jnp.clip(jax.random.normal(key_field, (CHAIN_LENGTH, CHAIN_LENGTH, C_Z), jnp.float32), -6.0, 6.0)
    strength = 110.0 * jnp.ones((MODULE_REPEATS, 1, ATTENTION_GROUPS), jnp.float32)
    weights = directions * (strength / C_Z) + rest
    coords = jnp.einsum('ijc,ck->ijk', field, basis)
    field = field - 0.9 * jnp.einsum('ijk,ck->ijc', coords, basis)
    field = jnp.clip(field, -24.0, 24.0)
    picks = jax.random.permutation(key_rows, CHAIN_LENGTH)
    for block_id in range(MODULE_REPEATS):
        for head_id in range(ATTENTION_GROUPS):
            slot = block_id * ATTENTION_GROUPS + head_id
            direction = directions[block_id, :, head_id]
            noise = jax.random.normal(jax.random.fold_in(key_noise, slot), (2, CHAIN_LENGTH, C_Z), jnp.float32)
            high_row = picks[2 * slot]
            low_row = picks[2 * slot + 1]
            field = field.at[high_row].set(jnp.clip(6.0 * direction[None, :] + 0.3 * noise[0], -24.0, 24.0))
            field = field.at[low_row].set(jnp.clip(-6.0 * direction[None, :] + 0.3 * noise[1], -24.0, 24.0))
    return (weights, field)


def draw_contact_matrix(key, part):
    return pair_law(key)[1].astype(jnp.bfloat16)


def draw_mixing_logit_matrix(key, part):
    return pair_law(key)[0].astype(jnp.bfloat16)


def level_of(key, dims, cuts, low, largest):
    factor_of = 1.0
    for position, parts in cuts:
        draws = jax.random.uniform(jax.random.fold_in(jax.random.fold_in(key, 6), position), (parts,), jnp.float32, low / len(cuts), largest / len(cuts))
        factor_of = factor_of * jnp.repeat(jnp.exp(draws), dims[position] // parts).reshape((-1,) + (1,) * (len(dims) - 1 - position))
    return factor_of


def gaussian(rng, dims, scale, limit, cuts=(), kind=jnp.bfloat16):
    entries = scale * jax.random.normal(rng, dims, jnp.float32)
    if cuts:
        entries = entries * level_of(rng, dims, cuts, -0.22, 0.18)
    return jnp.clip(entries, -limit, limit).astype(kind)


def setup_inputs(seed: int = 0) -> dict:
    arg_keys = jax.random.split(jax.random.key(seed), 12)
    return {
        "homolog_matrix": gaussian(arg_keys[0], (HOMOLOG_TOTAL, CHAIN_LENGTH, ALIGNED_FEATURES), 1.0, 6.0, ((0, 16), (1, 16))),
        "contact_matrix": draw_contact_matrix(jax.random.fold_in(arg_keys[11], 71), 0),
        "genuine_homolog_total": jax.random.randint(arg_keys[2], (1,), 1, HOMOLOG_TOTAL + 1).astype(jnp.int32),
        "genuine_chain_length": jax.random.randint(arg_keys[3], (1,), CHAIN_LENGTH // 2, CHAIN_LENGTH + 1).astype(jnp.int32),
        "tensor_product_matrices": gaussian(arg_keys[4], (MODULE_REPEATS, ALIGNED_FEATURES, 2 * PRODUCT_FEATURES), ALIGNED_FEATURES ** -0.5, 0.75),
        "tensor_product_final": gaussian(arg_keys[5], (MODULE_REPEATS, PRODUCT_FEATURES * PRODUCT_FEATURES, C_Z), (PRODUCT_FEATURES * PRODUCT_FEATURES // 16) ** -0.5, 0.75),
        "mixing_value_gate_matrix": gaussian(arg_keys[6], (MODULE_REPEATS, ALIGNED_FEATURES, 2 * ATTENTION_GROUPS * GROUP_FEATURES), ALIGNED_FEATURES ** -0.5, 0.75),
        "mixing_logit_matrix": draw_mixing_logit_matrix(jax.random.fold_in(arg_keys[11], 71), 0),
        "mixing_final_matrix": gaussian(arg_keys[8], (MODULE_REPEATS, ATTENTION_GROUPS * GROUP_FEATURES, ALIGNED_FEATURES), (ATTENTION_GROUPS * GROUP_FEATURES // 16) ** -0.5, 1.5),
        "feedforward_gate_expand": gaussian(arg_keys[9], (MODULE_REPEATS, C_Z, 2 * TRANS), C_Z ** -0.5, 0.5),
        "feedforward_shrink_matrix": gaussian(arg_keys[10], (MODULE_REPEATS, TRANS, C_Z), TRANS ** -0.5, 0.25),
    }


EPSILON = 1e-05
MASKED = -1000000000.0

def standardize_features(field):
    field = field.astype(jnp.float32)
    center = field - lax.optimization_barrier(jnp.mean(field, axis=-1, keepdims=True))
    spread = lax.optimization_barrier(jnp.mean(center * center, axis=-1, keepdims=True))
    return center * lax.rsqrt(spread + EPSILON)

def reference(homolog_matrix, contact_matrix, genuine_homolog_total, genuine_chain_length, tensor_product_matrices, tensor_product_final, mixing_value_gate_matrix, mixing_logit_matrix, mixing_final_matrix, feedforward_gate_expand, feedforward_shrink_matrix):
    hidden_width = ATTENTION_GROUPS * GROUP_FEATURES
    row_blocks = CHAIN_LENGTH // 8
    seq_float = (jnp.arange(HOMOLOG_TOTAL, dtype=jnp.int32) < genuine_homolog_total[0]).astype(jnp.float32)
    res_valid = jnp.arange(CHAIN_LENGTH, dtype=jnp.int32) < genuine_chain_length[0]
    res_float = res_valid.astype(jnp.float32)
    divisor = jnp.maximum(genuine_homolog_total[0].astype(jnp.float32) * res_float[:, None] * res_float[None, :], 1.0)
    starts = jnp.arange(row_blocks, dtype=jnp.int32) * 8
    for block_id in range(MODULE_REPEATS):
        standardized_source = standardize_features(homolog_matrix).astype(jnp.bfloat16)
        reshaped_tensor = standardized_source.reshape(HOMOLOG_TOTAL * CHAIN_LENGTH, ALIGNED_FEATURES)
        projected = jnp.dot(reshaped_tensor.astype(jnp.float32), tensor_product_matrices[block_id].astype(jnp.float32), preferred_element_type=jnp.float32).reshape(HOMOLOG_TOTAL, CHAIN_LENGTH, 2 * PRODUCT_FEATURES)
        projected = (projected * (seq_float[:, None, None] * res_float[None, :, None])).astype(jnp.bfloat16)
        left = projected[:, :, :PRODUCT_FEATURES]
        right = projected[:, :, PRODUCT_FEATURES:].reshape(HOMOLOG_TOTAL, CHAIN_LENGTH * PRODUCT_FEATURES)
        outer_weight = tensor_product_final[block_id]

        def outer_rows(inputs):
            start, pair_rows = inputs
            rows = lax.dynamic_slice_in_dim(left, start, 8, 1).reshape(HOMOLOG_TOTAL, 8 * PRODUCT_FEATURES)
            product = lax.dot_general(rows.astype(jnp.float32), right.astype(jnp.float32), (((0,), (0,)), ((), ())), preferred_element_type=jnp.float32)
            product = product.reshape(8, PRODUCT_FEATURES, CHAIN_LENGTH, PRODUCT_FEATURES).transpose(0, 2, 1, 3).reshape(8, CHAIN_LENGTH, PRODUCT_FEATURES * PRODUCT_FEATURES)
            scale = lax.dynamic_slice_in_dim(divisor, start, 8, 0)
            outer = (product / scale[:, :, None]).astype(jnp.bfloat16)
            update = jnp.dot(outer.reshape(8 * CHAIN_LENGTH, PRODUCT_FEATURES * PRODUCT_FEATURES).astype(jnp.float32), outer_weight.astype(jnp.float32), preferred_element_type=jnp.float32)
            return (pair_rows.astype(jnp.float32) + update.reshape(8, CHAIN_LENGTH, C_Z)).astype(jnp.bfloat16)
        contact_matrix = lax.map(outer_rows, (starts, contact_matrix.reshape(row_blocks, 8, CHAIN_LENGTH, C_Z))).reshape(CHAIN_LENGTH, CHAIN_LENGTH, C_Z)
        bias_weight = mixing_logit_matrix[block_id]

        def norm_rows(pair_rows):
            normed_rows = standardize_features(pair_rows).astype(jnp.bfloat16)
            logit_rows = jnp.dot(normed_rows.reshape(8 * CHAIN_LENGTH, C_Z).astype(jnp.float32), bias_weight.astype(jnp.float32), preferred_element_type=jnp.float32)
            return (normed_rows, logit_rows.reshape(8, CHAIN_LENGTH, ATTENTION_GROUPS))
        pair_normed, logits = lax.map(norm_rows, contact_matrix.reshape(row_blocks, 8, CHAIN_LENGTH, C_Z))
        logits = jnp.where(res_valid[None, :, None], logits.reshape(CHAIN_LENGTH, CHAIN_LENGTH, ATTENTION_GROUPS), MASKED)
        peak = lax.optimization_barrier(jnp.max(logits, axis=1, keepdims=True))
        expo = jnp.exp(logits - peak)
        weights = (expo / lax.optimization_barrier(jnp.sum(expo, axis=1, keepdims=True))).astype(jnp.bfloat16)
        both = jnp.dot(reshaped_tensor.astype(jnp.float32), mixing_value_gate_matrix[block_id].astype(jnp.float32), preferred_element_type=jnp.float32).reshape(HOMOLOG_TOTAL, CHAIN_LENGTH, 2 * hidden_width)
        values = both[:, :, :hidden_width].astype(jnp.bfloat16).reshape(HOMOLOG_TOTAL, CHAIN_LENGTH, ATTENTION_GROUPS, GROUP_FEATURES)
        gate = jax.nn.sigmoid(both[:, :, hidden_width:])
        averaged = jnp.einsum('ijh,sjhc->sihc', weights.astype(jnp.float32), values.astype(jnp.float32))
        gated = (gate * averaged.reshape(HOMOLOG_TOTAL, CHAIN_LENGTH, hidden_width)).astype(jnp.bfloat16)
        contact_increment = jnp.dot(gated.reshape(HOMOLOG_TOTAL * CHAIN_LENGTH, hidden_width).astype(jnp.float32), mixing_final_matrix[block_id].astype(jnp.float32), preferred_element_type=jnp.float32)
        homolog_matrix = (homolog_matrix.astype(jnp.float32) + contact_increment.reshape(HOMOLOG_TOTAL, CHAIN_LENGTH, ALIGNED_FEATURES)).astype(jnp.bfloat16)
        up_weight = feedforward_gate_expand[block_id]
        down_weight = feedforward_shrink_matrix[block_id]

        def transition_rows(inputs):
            pair_rows, normed_rows = inputs
            hidden = jnp.dot(normed_rows.reshape(8 * CHAIN_LENGTH, C_Z).astype(jnp.float32), up_weight.astype(jnp.float32), preferred_element_type=jnp.float32)
            active = (jax.nn.silu(hidden[:, :TRANS]) * hidden[:, TRANS:]).astype(jnp.bfloat16)
            update = jnp.dot(active.astype(jnp.float32), down_weight.astype(jnp.float32), preferred_element_type=jnp.float32)
            return (pair_rows.astype(jnp.float32) + update.reshape(8, CHAIN_LENGTH, C_Z)).astype(jnp.bfloat16)
        contact_matrix = lax.map(transition_rows, (contact_matrix.reshape(row_blocks, 8, CHAIN_LENGTH, C_Z), pair_normed)).reshape(CHAIN_LENGTH, CHAIN_LENGTH, C_Z)
    return (homolog_matrix, contact_matrix)
```

```python
import jax
import jax.numpy as jnp
from jax import lax
from jax.experimental import pallas as pl
from jax.experimental.pallas import tpu as pltpu

F32 = jnp.float32
BF = jnp.bfloat16


def normalize(field):
    center = field - jnp.mean(field, axis=-1, keepdims=True)
    spread = jnp.mean(center * center, axis=-1, keepdims=True)
    return center * lax.rsqrt(spread + 1e-5)


def full(shape):
    return pl.BlockSpec(shape, lambda *_: (0,) * len(shape))


def prologue_body(scal, homolog, left_weight, right_weight, normed_out, left_out, right_out, left_rows, right_rows):
    normed = normalize(homolog[...].astype(F32)).astype(BF)
    normed_out[...] = jnp.concatenate([normed[s] for s in range(8)], axis=1)
    projected = jnp.dot(normed.reshape(640, 64), left_weight[...], preferred_element_type=F32)
    left_rows[...] = projected.reshape(8, 80, 128)
    lane = lax.broadcasted_iota(jnp.int32, (8, 128), 1)
    seq_ok = scal[2] + lax.broadcasted_iota(jnp.int32, (8, 128), 0) < scal[0]
    group = lane // 32
    for q in range(20):
        piece = left_rows[:, 4 * q, :]
        for k in range(1, 4):
            piece = jnp.where(group == k, left_rows[:, 4 * q + k, :], piece)
        ok = seq_ok & (scal[3] + 4 * q + group < scal[1])
        left_out[:, q * 128 : (q + 1) * 128] = jnp.where(ok, piece, 0.0).astype(BF)
    for s in range(8):
        rows = jnp.concatenate([normed[s], jnp.zeros((48, 64), BF)], axis=0)
        right_rows[s] = lax.dot_general(
            right_weight[...], rows, (((1,), (1,)), ((), ())), preferred_element_type=F32
        )
    ok = seq_ok & (scal[3] + lane < scal[1])
    pieces = [jnp.where(ok, right_rows[:, d, :], 0.0)[:, :80] for d in range(32)]
    right_out[...] = jnp.concatenate(pieces, axis=1).astype(BF)


def prologue(scal, homolog, left_weight, right_weight):
    return pl.pallas_call(
        prologue_body,
        grid_spec=pltpu.PrefetchScalarGridSpec(
            num_scalar_prefetch=1,
            grid=(1,),
            in_specs=[full((8, 80, 64)), full((64, 128)), full((32, 64))],
            out_specs=[full((80, 512)), full((8, 2560)), full((8, 2560))],
            scratch_shapes=[pltpu.VMEM((8, 80, 128), F32), pltpu.VMEM((8, 32, 128), F32)],
        ),
        out_shape=[
            jax.ShapeDtypeStruct((80, 512), BF),
            jax.ShapeDtypeStruct((8, 2560), BF),
            jax.ShapeDtypeStruct((8, 2560), BF),
        ],
        name="prologue",
    )(scal, homolog, left_weight, right_weight)


def transition_body(contact, up_weight, down_weight, out):
    rows = contact[...].astype(F32)
    normed = normalize(rows).astype(BF)
    hidden = jnp.dot(normed, up_weight[...], preferred_element_type=F32)
    gate = hidden[:, :512]
    active = (gate * jax.nn.sigmoid(gate) * hidden[:, 512:]).astype(BF)
    out[...] = (rows + jnp.dot(active, down_weight[...], preferred_element_type=F32)).astype(BF)


def transition(contact, up_weight, down_weight):
    return pl.pallas_call(
        transition_body,
        grid=(10,),
        in_specs=[pl.BlockSpec((640, 128), lambda g: (g, 0)), full((128, 1024)), full((512, 128))],
        out_specs=pl.BlockSpec((640, 128), lambda g: (g, 0)),
        out_shape=jax.ShapeDtypeStruct((6400, 128), BF),
        compiler_params=pltpu.CompilerParams(vmem_limit_bytes=32 * 1024 * 1024),
        cost_estimate=pl.CostEstimate(flops=6400 * 128 * 1024 * 3, bytes_accessed=3300000, transcendentals=6400 * 512),
        name="transition",
    )(contact, up_weight, down_weight)


def average_body(weights, everyone, normed, homolog, value_weight, gate_weight, final_weight, out, scaled):
    def stat(a, k):
        return jnp.sum(weights[a, 80:96, :].astype(F32)[k : k + 3], axis=0, keepdims=True)

    peaks = [stat(a, 0) for a in range(16)]
    peak = peaks[0]
    for a in range(1, 16):
        peak = jnp.maximum(peak, peaks[a])
    factors = [jnp.exp(p - peak) for p in peaks]
    total = factors[0] * stat(0, 3)
    for a in range(1, 16):
        total = total + factors[a] * stat(a, 3)
    for a in range(16):
        scaled[a * 80 : (a + 1) * 80, :] = (weights[a, :80, :].astype(F32) * (factors[a] / total)).astype(BF)
    mixed = lax.dot_general(
        scaled[...], everyone[...], (((0,), (0,)), ((), ())), preferred_element_type=F32
    ).astype(BF)
    own = normed[...]
    sums = [None, None]
    for h in range(8):
        for q in range(2):
            value = jnp.dot(mixed[h * 80 : (h + 1) * 80, q * 256 : (q + 1) * 256], value_weight[h], preferred_element_type=F32)
            gate = jnp.dot(own[:, q * 256 : (q + 1) * 256], gate_weight[h], preferred_element_type=F32)
            gated = (jax.nn.sigmoid(gate) * value).astype(BF)
            term = jnp.dot(gated, final_weight[h], preferred_element_type=F32)
            sums[q] = term if sums[q] is None else sums[q] + term
    for s in range(8):
        out[s] = (homolog[s].astype(F32) + sums[s // 4][:, (s % 4) * 64 : (s % 4 + 1) * 64]).astype(BF)


def average(weights, everyone, normed, homolog, value_weight, gate_weight, final_weight):
    return pl.pallas_call(
        average_body,
        grid=(1,),
        in_specs=[
            full((16, 96, 640)), full((1280, 512)), full((80, 512)), full((8, 80, 64)),
            full((8, 256, 128)), full((8, 256, 128)), full((8, 128, 256)),
        ],
        out_specs=full((8, 80, 64)),
        out_shape=jax.ShapeDtypeStruct((8, 80, 64), BF),
        scratch_shapes=[pltpu.VMEM((1280, 640), BF)],
        compiler_params=pltpu.CompilerParams(vmem_limit_bytes=48 * 1024 * 1024),
        name="average",
    )(weights, everyone, normed, homolog, value_weight, gate_weight, final_weight)


ROWS = 8


def outer_body(scal, left, right, contact, final_weight, logit_weight, contact_out, weights_out, left_t, right_p, products, expo):
    step = pl.program_id(0)

    @pl.when(step == 0)
    def _():
        left_t[...] = jnp.transpose(left[...].astype(F32).reshape(128, 2560)).astype(BF)
        rows = right[...].astype(F32).reshape(128, 2560)
        for d in range(32):
            right_p[:, d * 128 : d * 128 + 80] = rows[:, d * 80 : (d + 1) * 80].astype(BF)
            right_p[:, d * 128 + 80 : (d + 1) * 128] = jnp.zeros((128, 48), BF)

    inverse = 1.0 / scal[0].astype(F32)
    lane = lax.broadcasted_iota(jnp.int32, (8, 128), 1)
    real = scal[3] + lane < scal[1]
    rows = left_t[pl.ds(pl.multiple_of(step * 256, 256), 256), :]
    for n in range(8):
        product = jnp.dot(rows, right_p[:, n * 512 : (n + 1) * 512], preferred_element_type=F32)
        product = (product * inverse).astype(BF)
        for i in range(ROWS):
            for q in range(4):
                d = n * 4 + q
                products[d * 32 : (d + 1) * 32, i * 128 : (i + 1) * 128] = product[
                    i * 32 : (i + 1) * 32, q * 128 : (q + 1) * 128
                ]
    for i in range(ROWS):
        if i % 2 == 0:
            update = jnp.dot(
                final_weight[...], products[:, i * 128 : (i + 2) * 128], preferred_element_type=F32
            )
        mine = jnp.transpose(update[:, (i % 2) * 128 : (i % 2 + 1) * 128])[:80]
        fresh = (contact[i].astype(F32) + mine).astype(BF)
        contact_out[i] = fresh
        normed = normalize(fresh.astype(F32)).astype(BF)
        normed = jnp.concatenate([normed, jnp.zeros((48, 128), BF)], axis=0)
        logits = lax.dot_general(
            logit_weight[...], normed, (((1,), (1,)), ((), ())), preferred_element_type=F32
        )
        logits = jnp.where(real, logits, -1e9)
        peak = jnp.max(jnp.where(lane < 80, logits, -3e38), axis=-1, keepdims=True)
        terms = jnp.where(lane < 80, jnp.exp(logits - peak), 0.0)
        total = jnp.sum(terms, axis=-1, keepdims=True)
        for k, value in enumerate((peak, total)):
            high = value.astype(BF).astype(F32)
            middle = (value - high).astype(BF).astype(F32)
            for t, part in enumerate((high, middle, value - high - middle)):
                terms = jnp.where(lane == 80 + 3 * k + t, part, terms)
        expo[:, pl.ds(step * ROWS + i, 1), :] = terms[:, None, :]

    @pl.when(step == 80 // ROWS - 1)
    def _():
        weights_out[...] = jnp.transpose(expo[...].reshape(640, 128))[:96].astype(BF)


def outer(scal, left, right, contact, final_weight, logit_weight):
    return pl.pallas_call(
        outer_body,
        grid_spec=pltpu.PrefetchScalarGridSpec(
            num_scalar_prefetch=1,
            grid=(80 // ROWS,),
            in_specs=[
                full((16, 8, 2560)), full((16, 8, 2560)),
                pl.BlockSpec((ROWS, 80, 128), lambda g, s: (g, 0, 0)),
                full((128, 1024)), full((8, 128)),
            ],
            out_specs=[pl.BlockSpec((ROWS, 80, 128), lambda g, s: (g, 0, 0)), full((96, 640))],
            scratch_shapes=[
                pltpu.VMEM((2560, 128), BF), pltpu.VMEM((128, 4096), BF),
                pltpu.VMEM((1024, 1024), BF), pltpu.VMEM((8, 80, 128), F32),
            ],
        ),
        out_shape=[jax.ShapeDtypeStruct((80, 80, 128), BF), jax.ShapeDtypeStruct((96, 640), BF)],
        compiler_params=pltpu.CompilerParams(vmem_limit_bytes=48 * 1024 * 1024),
        name="outer",
    )(scal, left, right, contact, final_weight, logit_weight)


def from_everyone(value, axis):
    return lax.all_to_all(
        jnp.broadcast_to(value[None], (lax.axis_size(axis), *value.shape)), axis, 0, 0, tiled=True
    )


def mirrored(value):
    size = lax.axis_size("row")
    pairs = [(r * size + c, c * size + r) for r in range(size) for c in range(size)]
    return lax.ppermute(value, ("row", "col"), pairs)


def spread(weight):
    heads, rows, columns = weight.shape
    eye = jnp.eye(4, dtype=weight.dtype)
    return (eye[None, :, None, :, None] * weight[:, None, :, None, :]).reshape(heads, 4 * rows, 4 * columns)


def local(
    homolog_matrix,
    contact_matrix,
    genuine_homolog_total,
    genuine_chain_length,
    tensor_product_matrices,
    tensor_product_final,
    mixing_value_gate_matrix,
    mixing_logit_matrix,
    mixing_final_matrix,
    feedforward_gate_expand,
    feedforward_shrink_matrix,
):
    row_index = lax.axis_index("row")
    col_index = lax.axis_index("col")
    scal = jnp.stack(
        [genuine_homolog_total[0], genuine_chain_length[0], row_index * 8, col_index * 80]
    ).astype(jnp.int32)
    left_weight = jnp.tile(tensor_product_matrices[0][:, :32], (1, 4))
    right_weight = tensor_product_matrices[0][:, 32:].T
    normed, left, right = prologue(scal, homolog_matrix, left_weight, right_weight)
    left = from_everyone(mirrored(left), "col")
    right = from_everyone(right, "row")
    everyone = lax.all_gather(normed, "col", tiled=True)
    final_weight = tensor_product_final[0].reshape(32, 32, 128).transpose(2, 1, 0).reshape(128, 1024)
    both = mixing_value_gate_matrix[0].reshape(64, 2, 8, 32).transpose(1, 2, 0, 3)
    value_weight = spread(both[0])
    gate_weight = spread(both[1])
    mixing_final = spread(mixing_final_matrix[0].reshape(8, 32, 64))
    contact, weights = outer(scal, left, right, contact_matrix, final_weight, mixing_logit_matrix[0].T)
    weights = from_everyone(mirrored(weights), "row")
    pair = transition(contact.reshape(6400, 128), feedforward_gate_expand[0], feedforward_shrink_matrix[0])
    msa = average(weights, everyone, normed, homolog_matrix, value_weight, gate_weight, mixing_final)
    return msa, pair.reshape(80, 80, 128)


def solution(mesh):
    split = jax.sharding.PartitionSpec("row", "col", None)
    whole = jax.sharding.PartitionSpec()
    return jax.shard_map(
        local, mesh=mesh, in_specs=(split, split) + (whole,) * 9, out_specs=(split, split), check_vma=False
    )
```

```python
import jax
import jax.numpy as jnp
from jax import lax
from jax.experimental import pallas as pl
from jax.experimental.pallas import tpu as pltpu

F32 = jnp.float32
BF = jnp.bfloat16
ROWS = 16


def normalize(field, axis=-1):
    center = field - jnp.mean(field, axis=axis, keepdims=True)
    spread = jnp.mean(center * center, axis=axis, keepdims=True)
    return center * lax.rsqrt(spread + 1e-5)


def full(shape):
    return pl.BlockSpec(shape, lambda *_: (0,) * len(shape))


def wide(value, lanes):
    missing = jnp.zeros((*value.shape[:-1], lanes - value.shape[-1]), value.dtype)
    return jnp.concatenate([value, missing], axis=-1)


def tall(value, rows):
    missing = jnp.zeros((rows - value.shape[0], *value.shape[1:]), value.dtype)
    return jnp.concatenate([value, missing], axis=0)


def call(body, scalars, grid, in_specs, out_specs, out_shape, scratch, cost, limit=48):
    flops, moved, special = cost
    return pl.pallas_call(
        body,
        grid_spec=pltpu.PrefetchScalarGridSpec(
            num_scalar_prefetch=scalars, grid=grid, in_specs=in_specs, out_specs=out_specs, scratch_shapes=scratch
        ),
        out_shape=out_shape,
        compiler_params=pltpu.CompilerParams(vmem_limit_bytes=limit * 1024 * 1024),
        cost_estimate=pl.CostEstimate(flops=flops, bytes_accessed=moved, transcendentals=special),
        name=body.__name__,
    )


def shaped(dtype, *dims):
    return jax.ShapeDtypeStruct(dims, dtype)


def prologue_body(seqs, residues, homolog, weight, left_out, shared_out, left_rows, right_rows):
    row, col = lax.axis_index("row"), lax.axis_index("col")
    normed = normalize(homolog[...].astype(F32), 1)
    rounded = normed.astype(BF)
    weights = weight[...].astype(F32)
    left_weight = jnp.concatenate([weights[:, :32]] * 4, axis=1).astype(BF)
    right_weight = jnp.transpose(wide(weights, 128))[32:64].astype(BF)
    for s in range(8):
        right_rows[s] = wide(jnp.dot(right_weight, rounded[s], preferred_element_type=F32), 128)
    turned = jnp.transpose(wide(normed.reshape(512, 80), 128))[:80].astype(BF)
    for k in range(5):
        shared_out[:16, k * 512 : (k + 1) * 512] = turned[k * 16 : (k + 1) * 16]
    for s in range(8):
        left_rows[s] = jnp.dot(turned[:, s * 64 : (s + 1) * 64], left_weight, preferred_element_type=F32)
    lane = lax.broadcasted_iota(jnp.int32, (8, 128), 1)
    seq_ok = row * 8 + lax.broadcasted_iota(jnp.int32, (8, 128), 0) < seqs[0]
    group = lane // 32
    for q in range(20):
        piece = left_rows[:, 4 * q, :]
        for k in range(1, 4):
            piece = jnp.where(group == k, left_rows[:, 4 * q + k, :], piece)
        ok = seq_ok & (col * 80 + 4 * q + group < residues[0])
        left_out[:, q * 128 : (q + 1) * 128] = jnp.where(ok, piece, 0.0).astype(BF)
    ok = seq_ok & (col * 80 + lane < residues[0])
    pieces = [jnp.where(ok, right_rows[:, d, :], 0.0)[:, :80] for d in range(32)]
    shared_out[16:, :] = jnp.concatenate(pieces, axis=1).astype(BF)


def prologue(seqs, residues, homolog, weight):
    return call(
        prologue_body, 2, (1,),
        [full((8, 64, 80)), full((64, 64))],
        [full((8, 2560)), full((24, 2560))],
        [shaped(BF, 8, 2560), shaped(BF, 24, 2560)],
        [pltpu.VMEM((8, 80, 128), F32), pltpu.VMEM((8, 32, 128), F32)],
        (10**8, 4 * 10**5, 10**4),
    )(seqs, residues, homolog, weight)


def weights_body(product, value_gate, mixing, product_out, value_out, gate_out, mixing_out, rows):
    rows[...] = product[...].astype(F32).reshape(32, 32, 128)
    swapped = jnp.concatenate([rows[:, d, :] for d in range(32)], axis=0)
    product_out[...] = jnp.transpose(swapped).astype(BF)
    value_out[...] = jnp.zeros_like(value_out)
    gate_out[...] = jnp.zeros_like(gate_out)
    mixing_out[...] = jnp.zeros_like(mixing_out)
    both = value_gate[...]
    final = jnp.transpose(tall(mixing[...].astype(F32), 128))[:, :64].astype(BF)
    for h in range(8):
        for s in range(4):
            value_out[h, s * 64 : (s + 1) * 64, s * 32 : (s + 1) * 32] = both[:, h * 32 : (h + 1) * 32]
            gate_out[h, s * 64 : (s + 1) * 64, s * 32 : (s + 1) * 32] = both[:, 256 + h * 32 : 288 + h * 32]
            mixing_out[h, s * 32 : (s + 1) * 32, s * 64 : (s + 1) * 64] = final[h * 32 : (h + 1) * 32]


def arrange_weights(product, value_gate, mixing):
    return call(
        weights_body, 0, (1,),
        [full((1024, 128)), full((64, 512)), full((64, 256))],
        [full((128, 1024)), full((8, 256, 128)), full((8, 256, 128)), full((8, 128, 256))],
        [shaped(BF, 128, 1024), shaped(BF, 8, 256, 128), shaped(BF, 8, 256, 128), shaped(BF, 8, 128, 256)],
        [pltpu.VMEM((32, 32, 128), F32)],
        (10**6, 2 * 10**6, 0),
    )(product, value_gate, mixing)


def outer_body(seqs, residues, left_a, left_b, right_a, right_b, right_c, right_d, contact, final_weight, logit_weight,
               contact_out, weights_out, left_t, right_p, products, expo, flat):
    step = pl.program_id(0)
    row, col = lax.axis_index("row"), lax.axis_index("col")

    @pl.when(step == 0)
    def _():
        for w, half in enumerate((left_a, left_b)):
            for v in range(4):
                for u in range(2):
                    flat[(w * 8 + v * 2 + u) * 8 : (w * 8 + v * 2 + u + 1) * 8, :] = half[v, u].astype(F32)
        left_t[...] = jnp.transpose(flat[...]).astype(BF)
        for m, part in enumerate((right_a, right_b, right_c, right_d)):
            for v in range(4):
                z = ((row >> 2) - v) & 3
                x = (row - m) & 3
                place = ((col ^ x) & 1) * 8 + (((col >> 2) - z) & 3) * 2 + (((col >> 1) ^ (x >> 1)) & 1)
                flat[pl.ds(pl.multiple_of(place * 8, 8), 8), :] = part[v].astype(F32)
        rows = flat[...]
        for d in range(32):
            right_p[:, d * 128 : (d + 1) * 128] = wide(rows[:, d * 80 : (d + 1) * 80], 128).astype(BF)

    inverse = 1.0 / seqs[0].astype(F32)
    lane = lax.broadcasted_iota(jnp.int32, (8 * ROWS, 128), 1)
    rows = left_t[pl.ds(pl.multiple_of(step * 32 * ROWS, 32 * ROWS), 32 * ROWS), :]
    for n in range(8):
        product = jnp.dot(rows, right_p[:, n * 512 : (n + 1) * 512], preferred_element_type=F32)
        product = (product * inverse).astype(BF)
        for i in range(ROWS):
            for q in range(4):
                d = n * 4 + q
                products[d * 32 : (d + 1) * 32, i * 128 : (i + 1) * 128] = product[
                    i * 32 : (i + 1) * 32, q * 128 : (q + 1) * 128
                ]
    updates = []
    for i in range(0, ROWS, 2):
        update = jnp.dot(final_weight[...], products[:, i * 128 : (i + 2) * 128], preferred_element_type=F32)
        updates += [jnp.transpose(update[:, :128])[:80], jnp.transpose(update[:, 128:])[:80]]
    fresh = contact[...].reshape(ROWS * 80, 128).astype(F32) + jnp.concatenate(updates, axis=0)
    fresh = fresh.astype(BF)
    contact_out[...] = fresh.reshape(ROWS, 80, 128)
    normed = normalize(fresh.astype(F32)).astype(BF)
    logits = jnp.concatenate(
        [
            lax.dot_general(
                logit_weight[...], tall(normed[i * 80 : (i + 1) * 80], 128), (((1,), (1,)), ((), ())),
                preferred_element_type=F32,
            )
            for i in range(ROWS)
        ],
        axis=0,
    )
    logits = jnp.where(col * 80 + lane < residues[0], logits, -1e9)
    peak = jnp.max(jnp.where(lane < 80, logits, -3e38), axis=-1, keepdims=True)
    terms = jnp.where(lane < 80, jnp.exp(logits - peak), 0.0)
    total = jnp.sum(terms, axis=-1, keepdims=True)
    for k, value in enumerate((peak, total)):
        high = value.astype(BF).astype(F32)
        middle = (value - high).astype(BF).astype(F32)
        for t, part in enumerate((high, middle, value - high - middle)):
            terms = jnp.where(lane == 80 + 3 * k + t, part, terms)
    expo[pl.ds(step * ROWS, ROWS)] = terms.reshape(ROWS, 8, 128)

    @pl.when(step == 80 // ROWS - 1)
    def _():
        for q in range(4):
            weights_out[q] = expo[pl.ds((((col >> 2) + q) & 3) * 20, 20)].reshape(160, 128).astype(BF)


def outer(seqs, residues, left, right, contact, final_weight, logit_weight):
    block = pl.BlockSpec((ROWS, 80, 128), lambda g, *_: (g, 0, 0))
    return call(
        outer_body, 2, (80 // ROWS,),
        [full((4, 2, 8, 2560))] * 2 + [full((4, 8, 2560))] * 4 + [block, full((128, 1024)), full((8, 128))],
        [block, full((4, 160, 128))],
        [shaped(BF, 80, 80, 128), shaped(BF, 4, 160, 128)],
        [
            pltpu.VMEM((2560, 128), BF), pltpu.VMEM((128, 4096), BF), pltpu.VMEM((1024, 128 * ROWS), BF),
            pltpu.VMEM((80, 8, 128), F32), pltpu.VMEM((128, 2560), F32),
        ],
        (12 * 10**9, 6 * 10**6, 10**5),
    )(seqs, residues, *left, *right, contact, final_weight, logit_weight)


def transition_body(contact, up_weight, down_weight, out):
    rows = contact[...].reshape(640, 128).astype(F32)
    normed = normalize(rows).astype(BF)
    hidden = jnp.dot(normed, up_weight[...], preferred_element_type=F32)
    gate = hidden[:, :512]
    active = (gate * jax.nn.sigmoid(gate) * hidden[:, 512:]).astype(BF)
    rows = rows + jnp.dot(active, down_weight[...], preferred_element_type=F32)
    out[...] = rows.astype(BF).reshape(8, 80, 128)


def transition(contact, up_weight, down_weight):
    block = pl.BlockSpec((8, 80, 128), lambda g: (g, 0, 0))
    return call(
        transition_body, 0, (10,),
        [block, full((128, 1024)), full((512, 128))],
        block, shaped(BF, 80, 80, 128), [],
        (5 * 10**9, 33 * 10**5, 6400 * 512), 32,
    )(contact, up_weight, down_weight)


def average_body(part_a, part_b, part_c, part_d, everyone_a, everyone_b, value_weight, gate_weight, final_weight,
                 out_a, out_b, out_c, out_d, scaled, mixed, normed):
    row, col = lax.axis_index("row"), lax.axis_index("col")
    parts = (part_a, part_b, part_c, part_d)
    blocks = [(x, z) for x in range(4) for z in range(4)]
    lane = lax.broadcasted_iota(jnp.int32, (160, 128), 1)

    def stat(x, z, k):
        here = (lane >= 80 + 3 * k) & (lane < 83 + 3 * k)
        return jnp.sum(jnp.where(here, parts[x][z].astype(F32), 0.0), axis=-1, keepdims=True)

    peaks = [stat(x, z, 0) for x, z in blocks]
    peak = peaks[0]
    for other in peaks[1:]:
        peak = jnp.maximum(peak, other)
    factors = [jnp.exp(p - peak) for p in peaks]
    total = sum(f * stat(x, z, 1) for f, (x, z) in zip(factors, blocks))
    inverse = 1.0 / total
    for factor, (x, z) in zip(factors, blocks):
        far_z = ((row >> 2) - z) & 3
        far_x = (row - x) & 3
        place = ((col ^ far_x) & 1) * 8 + (((col >> 2) - far_z) & 3) * 2 + (((col >> 1) ^ (far_x >> 1)) & 1)
        scaled[place] = parts[x][z].astype(F32) * (factor * inverse)
    for w, everyone in enumerate((everyone_a, everyone_b)):
        for v in range(4):
            for u in range(2):
                for k in range(5):
                    start = (w * 8 + v * 2 + u) * 80 + k * 16
                    for z in range(4):
                        normed[start : start + 16, z * 512 : (z + 1) * 512] = everyone[v, u, z, :, k * 512 : (k + 1) * 512]
    sums = None
    for w in range(2):
        rows = jnp.concatenate([scaled[w * 8 + k][:, :80] for k in range(8)], axis=1).astype(BF)
        term = jnp.dot(rows, normed[w * 640 : (w + 1) * 640, :], preferred_element_type=F32)
        sums = term if sums is None else sums + term
    mixed[...] = sums.reshape(20, 8, 2048)
    pick = lax.broadcasted_iota(jnp.int32, (24, 80), 1) - ((row >> 2) & 3) * 20
    pick = (pick == lax.broadcasted_iota(jnp.int32, (24, 80), 0)) & (pick < 20)
    own = jnp.dot(pick.astype(F32).astype(BF), normed[:80, :], preferred_element_type=F32)

    def stacked(value):
        return jnp.concatenate([value[:, g * 256 : (g + 1) * 256] for g in range(8)], axis=0).astype(BF)

    own = stacked(own)
    result = None
    for h in range(8):
        value = jnp.dot(stacked(tall(mixed[:, h, :], 24)), value_weight[h], preferred_element_type=F32)
        gate = jnp.dot(own, gate_weight[h], preferred_element_type=F32)
        gated = (jax.nn.sigmoid(gate) * value).astype(BF)
        term = jnp.dot(gated, final_weight[h], preferred_element_type=F32)
        result = term if result is None else result + term
    for v, out in enumerate((out_a, out_b, out_c, out_d)):
        out[...] = result[v * 48 : (v + 1) * 48]


def average(parts, everyone, value_weight, gate_weight, final_weight):
    return call(
        average_body, 0, (1,),
        [full((4, 160, 128))] * 4 + [full((4, 2, 4, 16, 2560))] * 2 + [
            full((8, 256, 128)), full((8, 256, 128)), full((8, 128, 256))
        ],
        [full((48, 256))] * 4, [shaped(F32, 48, 256)] * 4,
        [pltpu.VMEM((16, 160, 128), F32), pltpu.VMEM((20, 8, 2048), F32), pltpu.VMEM((1280, 2048), BF)],
        (3 * 10**9, 8 * 10**6, 10**5),
    )(*parts, *everyone, value_weight, gate_weight, final_weight)


def epilogue_body(part_a, part_b, part_c, part_d, homolog, out, pieces):
    row = lax.axis_index("row")
    for v, part in enumerate((part_a, part_b, part_c, part_d)):
        pieces[v] = part[...]
    for half in range(2):
        rows = jnp.concatenate(
            [pieces[(q - (row >> 2)) & 3][half * 24 : half * 24 + 20] for q in range(4)], axis=0
        )
        turned = jnp.transpose(tall(rows, 128))
        for s in range(4):
            fresh = homolog[half * 4 + s].astype(F32) + turned[s * 64 : (s + 1) * 64, :80]
            out[half * 4 + s] = fresh.astype(BF)


def epilogue(parts, homolog):
    return call(
        epilogue_body, 0, (1,),
        [full((48, 256))] * 4 + [full((8, 64, 80))], full((8, 64, 80)), shaped(BF, 8, 64, 80),
        [pltpu.VMEM((4, 48, 256), F32)],
        (10**6, 4 * 10**5, 0),
    )(*parts, homolog)


def place(z, x, y, h, core):
    return (z * 4 + x) * 16 + y * 4 + h * 2 + core


def route(value, target):
    pairs = []
    for index in range(256):
        row, col = divmod(index, 16)
        z, x, y, h, core = row >> 2, row & 3, col >> 2, (col >> 1) & 1, col & 1
        pairs.append((index, place(*target(z, x, y, h, core))))
    return lax.ppermute(value, ("row", "col"), pairs)


def along_x(value, m):
    return route(value, lambda z, x, y, h, c: (z, (x + m) % 4, y, h, c))


def along_z(value, m):
    return route(value, lambda z, x, y, h, c: ((z + m) % 4, x, y, h, c))


def along_y(value, m):
    return route(value, lambda z, x, y, h, c: (z, x, (y + m) % 4, h, c))


def along_x(value, m):
    return route(value, lambda z, x, y, h, c: (z, (x + m) % 4, y, h, c))


def along_z(value, m):
    return route(value, lambda z, x, y, h, c: ((z + m) % 4, x, y, h, c))


def along_y(value, m):
    return route(value, lambda z, x, y, h, c: (z, x, (y + m) % 4, h, c))


ALONG = {
    "x": ("row", [[4 * z + x for x in range(4)] for z in range(4)]),
    "z": ("row", [[4 * z + x for z in range(4)] for x in range(4)]),
    "y": ("col", [[4 * y + j for y in range(4)] for j in range(4)]),
}


def exchange(values, line):
    axis, groups = ALONG[line]
    return lax.all_to_all(values, axis, 0, 0, axis_index_groups=groups, tiled=True)


def from_line(value, line):
    return exchange(jnp.broadcast_to(value[None], (4, *value.shape)), line)


def across(value):
    return route(value, lambda z, x, y, h, c: (z, x, y, h ^ 1, c))


def core_swap(value):
    return route(value, lambda z, x, y, h, c: (z, x, y, h, c ^ 1))


def after(value, *others):
    return lax.optimization_barrier((value, *others))[0]


def local(
    homolog_matrix,
    contact_matrix,
    seqs,
    residues,
    tensor_product_matrices,
    tensor_product_final,
    mixing_value_gate_matrix,
    mixing_logit_matrix,
    mixing_final_matrix,
    feedforward_gate_expand,
    feedforward_shrink_matrix,
):
    homolog = jnp.swapaxes(homolog_matrix, 1, 2)
    left, shared = prologue(seqs, residues, homolog, tensor_product_matrices[0])
    product_weight, value_weight, gate_weight, mixing_weight = arrange_weights(
        tensor_product_final[0], mixing_value_gate_matrix[0], mixing_final_matrix[0].T
    )

    halves = jnp.stack([
        route(left, lambda z, x, y, h, c, u=u: (y, 2 * h + c, z, (x >> 1) ^ u, x & 1)) for u in range(2)
    ])
    shared = jnp.stack([shared] + [along_z(shared, m) for m in (1, 2, 3)])
    column = shared[:, 16:]
    left_half = jnp.stack([halves] + [along_y(halves, m) for m in (1, 2, 3)])
    right = [column] + [along_x(column, m) for m in (1, 3, 2)]
    right[2], right[3] = right[3], right[2]
    left_all = [left_half, core_swap(left_half)]
    group = after(shared[:, :16], *left_all, *right)
    group = jnp.stack([group, across(group)])

    contact, weights = outer(
        seqs, residues, left_all, right, contact_matrix, product_weight, mixing_logit_matrix[0].T
    )
    group = after(group, weights)
    behind, ahead = along_y(group, 1), along_y(group, 3)
    weights = route(weights, lambda z, x, y, h, c: (y, 2 * h + c, z, x >> 1, x & 1))
    pair = transition(contact, feedforward_gate_expand[0], feedforward_shrink_matrix[0])
    weights, behind, ahead, pair = lax.optimization_barrier((weights, behind, ahead, pair))
    weights = jnp.stack([weights[0]] + [along_z(weights[v], v) for v in (1, 2, 3)])
    opposite = jnp.stack([along_y(behind[0], 1), along_y(ahead[1], 3)])
    weights, opposite = lax.optimization_barrier((weights, opposite))
    weights = [weights] + [along_x(weights, m) for m in (1, 3, 2)]
    weights[2], weights[3] = weights[3], weights[2]
    everyone = jnp.stack([group, behind, opposite, ahead])
    everyone = [everyone, core_swap(everyone)]
    own, *others = average(weights, everyone, value_weight, gate_weight, mixing_weight)
    others = [along_z(part, 4 - v) for v, part in zip((1, 2, 3), others)]
    msa = epilogue([own] + others, homolog)
    return jnp.swapaxes(msa, 1, 2), pair


def solution(mesh):
    split = jax.sharding.PartitionSpec("row", "col", None)
    whole = jax.sharding.PartitionSpec()
    return jax.shard_map(
        local, mesh=mesh, in_specs=(split, split) + (whole,) * 9, out_specs=(split, split), check_vma=False
    )
```

```python
import jax
import jax.numpy as jnp
from jax import lax
from jax.experimental import pallas as pl
from jax.experimental.pallas import tpu as pltpu

F32 = jnp.float32
BF = jnp.bfloat16
ROWS = 16


def normalize(field, axis=-1):
    center = field - jnp.mean(field, axis=axis, keepdims=True)
    spread = jnp.mean(center * center, axis=axis, keepdims=True)
    return center * lax.rsqrt(spread + 1e-5)


def full(shape):
    return pl.BlockSpec(shape, lambda *_: (0,) * len(shape))


def wide(value, lanes):
    missing = jnp.zeros((*value.shape[:-1], lanes - value.shape[-1]), value.dtype)
    return jnp.concatenate([value, missing], axis=-1)


def tall(value, rows):
    missing = jnp.zeros((rows - value.shape[0], *value.shape[1:]), value.dtype)
    return jnp.concatenate([value, missing], axis=0)


def call(body, scalars, grid, in_specs, out_specs, out_shape, scratch, cost, limit=48):
    flops, moved, special = cost
    return pl.pallas_call(
        body,
        grid_spec=pltpu.PrefetchScalarGridSpec(
            num_scalar_prefetch=scalars, grid=grid, in_specs=in_specs, out_specs=out_specs, scratch_shapes=scratch
        ),
        out_shape=out_shape,
        compiler_params=pltpu.CompilerParams(vmem_limit_bytes=limit * 1024 * 1024),
        cost_estimate=pl.CostEstimate(flops=flops, bytes_accessed=moved, transcendentals=special),
        name=body.__name__,
    )


def shaped(dtype, *dims):
    return jax.ShapeDtypeStruct(dims, dtype)


def prologue_body(seqs, residues, homolog, weight, left_out, right_out, shared_out, left_rows, right_rows):
    row, col = lax.axis_index("row"), lax.axis_index("col")
    normed = normalize(homolog[...].astype(F32), 1)
    rounded = normed.astype(BF)
    weights = weight[...].astype(F32)
    left_weight = jnp.concatenate([weights[:, :32]] * 4, axis=1).astype(BF)
    right_weight = jnp.transpose(wide(weights, 128))[32:64].astype(BF)
    for s in range(8):
        right_rows[s] = wide(jnp.dot(right_weight, rounded[s], preferred_element_type=F32), 128)
    turned = jnp.transpose(wide(normed.reshape(512, 80), 128))[:80].astype(BF)
    for k in range(5):
        shared_out[:16, k * 512 : (k + 1) * 512] = turned[k * 16 : (k + 1) * 16]
    for s in range(8):
        left_rows[s] = jnp.dot(turned[:, s * 64 : (s + 1) * 64], left_weight, preferred_element_type=F32)
    lane = lax.broadcasted_iota(jnp.int32, (8, 128), 1)
    seq_ok = row * 8 + lax.broadcasted_iota(jnp.int32, (8, 128), 0) < seqs[0]
    group = lane // 32
    for q in range(20):
        piece = left_rows[:, 4 * q, :]
        for k in range(1, 4):
            piece = jnp.where(group == k, left_rows[:, 4 * q + k, :], piece)
        ok = seq_ok & (col * 80 + 4 * q + group < residues[0])
        left_out[:, q * 128 : (q + 1) * 128] = jnp.where(ok, piece, 0.0).astype(BF)
    ok = seq_ok & (col * 80 + lane < residues[0])
    pieces = [jnp.where(ok, right_rows[:, d, :], 0.0)[:, :80] for d in range(32)]
    pieces = jnp.concatenate(pieces, axis=1).astype(BF)
    right_out[...] = pieces
    shared_out[16:, :] = pieces


def prologue(seqs, residues, homolog, weight):
    return call(
        prologue_body, 2, (1,),
        [full((8, 64, 80)), full((64, 64))],
        [full((8, 2560)), full((8, 2560)), full((24, 2560))],
        [shaped(BF, 8, 2560), shaped(BF, 8, 2560), shaped(BF, 24, 2560)],
        [pltpu.VMEM((8, 80, 128), F32), pltpu.VMEM((8, 32, 128), F32)],
        (10**8, 4 * 10**5, 10**4),
    )(seqs, residues, homolog, weight)


def weights_body(product, value_gate, mixing, product_out, value_out, gate_out, mixing_out, rows):
    rows[...] = product[...].astype(F32).reshape(32, 32, 128)
    swapped = jnp.concatenate([rows[:, d, :] for d in range(32)], axis=0)
    product_out[...] = jnp.transpose(swapped).astype(BF)
    value_out[...] = jnp.zeros_like(value_out)
    gate_out[...] = jnp.zeros_like(gate_out)
    mixing_out[...] = jnp.zeros_like(mixing_out)
    both = value_gate[...]
    final = jnp.transpose(tall(mixing[...].astype(F32), 128))[:, :64].astype(BF)
    for h in range(8):
        for s in range(4):
            value_out[h, s * 64 : (s + 1) * 64, s * 32 : (s + 1) * 32] = both[:, h * 32 : (h + 1) * 32]
            gate_out[h, s * 64 : (s + 1) * 64, s * 32 : (s + 1) * 32] = both[:, 256 + h * 32 : 288 + h * 32]
            mixing_out[h, s * 32 : (s + 1) * 32, s * 64 : (s + 1) * 64] = final[h * 32 : (h + 1) * 32]


def arrange_weights(product, value_gate, mixing):
    return call(
        weights_body, 0, (1,),
        [full((1024, 128)), full((64, 512)), full((64, 256))],
        [full((128, 1024)), full((8, 256, 128)), full((8, 256, 128)), full((8, 128, 256))],
        [shaped(BF, 128, 1024), shaped(BF, 8, 256, 128), shaped(BF, 8, 256, 128), shaped(BF, 8, 128, 256)],
        [pltpu.VMEM((32, 32, 128), F32)],
        (10**6, 2 * 10**6, 0),
    )(product, value_gate, mixing)


def outer_body(seqs, residues, left_a, left_b, right_a, right_b, right_c, right_d, contact, final_weight, logit_weight,
               contact_out, weights_out, left_t, right_p, products, expo, flat):
    step = pl.program_id(0)
    row, col = lax.axis_index("row"), lax.axis_index("col")

    @pl.when(step == 0)
    def _():
        for w, half in enumerate((left_a, left_b)):
            for v in range(4):
                for u in range(2):
                    flat[(w * 8 + v * 2 + u) * 8 : (w * 8 + v * 2 + u + 1) * 8, :] = half[v, u].astype(F32)
        left_t[...] = jnp.transpose(flat[...]).astype(BF)
        for m, part in enumerate((right_a, right_b, right_c, right_d)):
            for v in range(4):
                z = (row >> 2) ^ v
                x = (row - m) & 3
                place = ((col ^ x) & 1) * 8 + (((col >> 2) - z) & 3) * 2 + (((col >> 1) ^ (x >> 1)) & 1)
                flat[pl.ds(pl.multiple_of(place * 8, 8), 8), :] = part[v].astype(F32)
        rows = flat[...]
        for d in range(32):
            right_p[:, d * 128 : (d + 1) * 128] = wide(rows[:, d * 80 : (d + 1) * 80], 128).astype(BF)

    inverse = 1.0 / seqs[0].astype(F32)
    lane = lax.broadcasted_iota(jnp.int32, (8 * ROWS, 128), 1)
    rows = left_t[pl.ds(pl.multiple_of(step * 32 * ROWS, 32 * ROWS), 32 * ROWS), :]
    for n in range(8):
        product = jnp.dot(rows, right_p[:, n * 512 : (n + 1) * 512], preferred_element_type=F32)
        product = (product * inverse).astype(BF)
        for i in range(ROWS):
            for q in range(4):
                d = n * 4 + q
                products[d * 32 : (d + 1) * 32, i * 128 : (i + 1) * 128] = product[
                    i * 32 : (i + 1) * 32, q * 128 : (q + 1) * 128
                ]
    updates = []
    for i in range(0, ROWS, 2):
        update = jnp.dot(final_weight[...], products[:, i * 128 : (i + 2) * 128], preferred_element_type=F32)
        updates += [jnp.transpose(update[:, :128])[:80], jnp.transpose(update[:, 128:])[:80]]
    fresh = contact[...].reshape(ROWS * 80, 128).astype(F32) + jnp.concatenate(updates, axis=0)
    fresh = fresh.astype(BF)
    contact_out[...] = fresh.reshape(ROWS, 80, 128)
    normed = normalize(fresh.astype(F32)).astype(BF)
    logits = jnp.concatenate(
        [
            lax.dot_general(
                logit_weight[...], tall(normed[i * 80 : (i + 1) * 80], 128), (((1,), (1,)), ((), ())),
                preferred_element_type=F32,
            )
            for i in range(ROWS)
        ],
        axis=0,
    )
    logits = jnp.where(col * 80 + lane < residues[0], logits, -1e9)
    peak = jnp.max(jnp.where(lane < 80, logits, -3e38), axis=-1, keepdims=True)
    terms = jnp.where(lane < 80, jnp.exp(logits - peak), 0.0)
    total = jnp.sum(terms, axis=-1, keepdims=True)
    for k, value in enumerate((peak, total)):
        high = value.astype(BF).astype(F32)
        middle = (value - high).astype(BF).astype(F32)
        for t, part in enumerate((high, middle, value - high - middle)):
            terms = jnp.where(lane == 80 + 3 * k + t, part, terms)
    expo[pl.ds(step * ROWS, ROWS)] = terms.reshape(ROWS, 8, 128)

    @pl.when(step == 80 // ROWS - 1)
    def _():
        for q in range(2):
            weights_out[q] = expo[pl.ds((((col >> 2) + q) & 1) * 40, 40)].reshape(320, 128).astype(BF)


def outer(seqs, residues, left, right, contact, final_weight, logit_weight):
    block = pl.BlockSpec((ROWS, 80, 128), lambda g, *_: (g, 0, 0))
    return call(
        outer_body, 2, (80 // ROWS,),
        [full((4, 2, 8, 2560))] * 2 + [full((4, 8, 2560))] * 4 + [block, full((128, 1024)), full((8, 128))],
        [block, full((2, 320, 128))],
        [shaped(BF, 80, 80, 128), shaped(BF, 2, 320, 128)],
        [
            pltpu.VMEM((2560, 128), BF), pltpu.VMEM((128, 4096), BF), pltpu.VMEM((1024, 128 * ROWS), BF),
            pltpu.VMEM((80, 8, 128), F32), pltpu.VMEM((128, 2560), F32),
        ],
        (12 * 10**9, 6 * 10**6, 10**5),
    )(seqs, residues, *left, *right, contact, final_weight, logit_weight)


def transition_body(contact, up_weight, down_weight, out):
    rows = contact[...].reshape(640, 128).astype(F32)
    normed = normalize(rows).astype(BF)
    hidden = jnp.dot(normed, up_weight[...], preferred_element_type=F32)
    gate = hidden[:, :512]
    active = (gate * jax.nn.sigmoid(gate) * hidden[:, 512:]).astype(BF)
    rows = rows + jnp.dot(active, down_weight[...], preferred_element_type=F32)
    out[...] = rows.astype(BF).reshape(8, 80, 128)


def transition(contact, up_weight, down_weight):
    block = pl.BlockSpec((8, 80, 128), lambda g: (g, 0, 0))
    return call(
        transition_body, 0, (10,),
        [block, full((128, 1024)), full((512, 128))],
        block, shaped(BF, 80, 80, 128), [],
        (5 * 10**9, 33 * 10**5, 6400 * 512), 32,
    )(contact, up_weight, down_weight)


def average_body(part_a, part_b, part_c, part_d, part_e, everyone_a, everyone_b, value_weight, gate_weight, final_weight,
                 out_a, out_b, scaled, mixed, normed):
    row, col = lax.axis_index("row"), lax.axis_index("col")
    parts = (part_a, part_b, (part_c.at[0], part_c.at[1], part_d.at[0], part_d.at[1]), part_e)
    blocks = [(x, z) for x in range(4) for z in range(4)]
    lane = lax.broadcasted_iota(jnp.int32, (320, 128), 1)

    def block(x, z):
        return (parts[x][z][...] if x == 2 else parts[x][z]).astype(F32)

    def stat(x, z, k):
        here = (lane >= 80 + 3 * k) & (lane < 83 + 3 * k)
        return jnp.sum(jnp.where(here, block(x, z), 0.0), axis=-1, keepdims=True)

    peaks = [stat(x, z, 0) for x, z in blocks]
    peak = peaks[0]
    for other in peaks[1:]:
        peak = jnp.maximum(peak, other)
    factors = [jnp.exp(p - peak) for p in peaks]
    total = sum(f * stat(x, z, 1) for f, (x, z) in zip(factors, blocks))
    inverse = 1.0 / total
    for factor, (x, z) in zip(factors, blocks):
        far_z = (row >> 2) ^ z
        far_x = (row - x) & 3
        place = ((col ^ far_x) & 1) * 8 + (((col >> 2) - far_z) & 3) * 2 + (((col >> 1) ^ (far_x >> 1)) & 1)
        scaled[place] = block(x, z) * (factor * inverse)
    for w, everyone in enumerate((everyone_a, everyone_b)):
        for v in range(4):
            for u in range(2):
                for k in range(5):
                    start = (w * 8 + v * 2 + u) * 80 + k * 16
                    for z in range(2):
                        normed[start : start + 16, z * 512 : (z + 1) * 512] = everyone[v, u, z, :, k * 512 : (k + 1) * 512]
    sums = None
    for w in range(2):
        rows = jnp.concatenate([scaled[w * 8 + k][:, :80] for k in range(8)], axis=1).astype(BF)
        term = jnp.dot(rows, normed[w * 640 : (w + 1) * 640, :], preferred_element_type=F32)
        sums = term if sums is None else sums + term
    mixed[...] = sums.reshape(40, 8, 1024)
    pick = lax.broadcasted_iota(jnp.int32, (40, 80), 1) - ((row >> 2) & 1) * 40
    pick = pick == lax.broadcasted_iota(jnp.int32, (40, 80), 0)
    own = jnp.dot(pick.astype(F32).astype(BF), normed[:80, :], preferred_element_type=F32)

    def stacked(value):
        return jnp.concatenate([value[:, g * 256 : (g + 1) * 256] for g in range(4)], axis=0).astype(BF)

    own = stacked(own)
    result = None
    for h in range(8):
        value = jnp.dot(stacked(mixed[:, h, :]), value_weight[h], preferred_element_type=F32)
        gate = jnp.dot(own, gate_weight[h], preferred_element_type=F32)
        gated = (jax.nn.sigmoid(gate) * value).astype(BF)
        term = jnp.dot(gated, final_weight[h], preferred_element_type=F32)
        result = term if result is None else result + term
    out_a[...] = result[:80]
    out_b[...] = result[80:]


def average(parts, everyone, value_weight, gate_weight, final_weight):
    return call(
        average_body, 0, (1,),
        [full((4, 320, 128))] * 2 + [full((2, 320, 128))] * 2 + [full((4, 320, 128))] + [full((4, 2, 2, 16, 2560))] * 2 + [
            full((8, 256, 128)), full((8, 256, 128)), full((8, 128, 256))
        ],
        [full((80, 256))] * 2, [shaped(F32, 80, 256)] * 2,
        [pltpu.VMEM((16, 320, 128), F32), pltpu.VMEM((40, 8, 1024), F32), pltpu.VMEM((1280, 1024), BF)],
        (3 * 10**9, 8 * 10**6, 10**5), 36,
    )(*parts, *everyone, value_weight, gate_weight, final_weight)


def epilogue_body(part_a, part_b, homolog, out, pieces):
    parity = (lax.axis_index("row") >> 2) & 1
    pieces[0] = part_a[...]
    pieces[1] = part_b[...]
    for half in range(2):
        rows = jnp.concatenate([pieces[parity ^ q][half * 40 : half * 40 + 40] for q in range(2)], axis=0)
        turned = jnp.transpose(tall(rows, 128))
        for s in range(4):
            fresh = homolog[half * 4 + s].astype(F32) + turned[s * 64 : (s + 1) * 64, :80]
            out[half * 4 + s] = fresh.astype(BF)


def epilogue(parts, homolog):
    return call(
        epilogue_body, 0, (1,),
        [full((80, 256))] * 2 + [full((8, 64, 80))], full((8, 64, 80)), shaped(BF, 8, 64, 80),
        [pltpu.VMEM((2, 80, 256), F32)],
        (10**6, 4 * 10**5, 0),
    )(*parts, homolog)


def place(z, x, y, h, core):
    return (z * 4 + x) * 16 + y * 4 + h * 2 + core


def route(value, target):
    pairs = []
    for index in range(256):
        row, col = divmod(index, 16)
        z, x, y, h, core = row >> 2, row & 3, col >> 2, (col >> 1) & 1, col & 1
        pairs.append((index, place(*target(z, x, y, h, core))))
    return lax.ppermute(value, ("row", "col"), pairs)


def along_x(value, m):
    return route(value, lambda z, x, y, h, c: (z, (x + m) % 4, y, h, c))


def along_z(value, m):
    return route(value, lambda z, x, y, h, c: (z ^ m, x, y, h, c))


def along_y(value, m):
    return route(value, lambda z, x, y, h, c: (z, x, (y + m) % 4, h, c))


ALONG = {
    "x": ("row", [[4 * z + x for x in range(4)] for z in range(4)]),
    "z": ("row", [[4 * z + x for z in range(4)] for x in range(4)]),
    "y": ("col", [[4 * y + j for y in range(4)] for j in range(4)]),
}


def exchange(values, line):
    axis, groups = ALONG[line]
    return lax.all_to_all(values, axis, 0, 0, axis_index_groups=groups, tiled=True)


def from_line(value, line):
    return exchange(jnp.broadcast_to(value[None], (4, *value.shape)), line)


def across(value):
    return route(value, lambda z, x, y, h, c: (z, x, y, h ^ 1, c))


def core_swap(value):
    return route(value, lambda z, x, y, h, c: (z, x, y, h, c ^ 1))


def after(value, *others):
    return lax.optimization_barrier((value, *others))[0]


def local(
    homolog_matrix,
    contact_matrix,
    seqs,
    residues,
    tensor_product_matrices,
    tensor_product_final,
    mixing_value_gate_matrix,
    mixing_logit_matrix,
    mixing_final_matrix,
    feedforward_gate_expand,
    feedforward_shrink_matrix,
):
    homolog = jnp.swapaxes(homolog_matrix, 1, 2)
    left, right, shared = prologue(seqs, residues, homolog, tensor_product_matrices[0])
    product_weight, value_weight, gate_weight, mixing_weight = arrange_weights(
        tensor_product_final[0], mixing_value_gate_matrix[0], mixing_final_matrix[0].T
    )

    halves = jnp.stack([
        route(left, lambda z, x, y, h, c, u=u: (y, 2 * h + c, z, (x >> 1) ^ u, x & 1)) for u in range(2)
    ])
    partner = along_z(shared, 1)
    column = jnp.stack([right, partner[16:]] + [along_z(right, m) for m in (2, 3)])
    left_half = jnp.stack([halves] + [along_y(halves, m) for m in (1, 2, 3)])
    right = [column] + [along_x(column, m) for m in (1, 3, 2)]
    right[2], right[3] = right[3], right[2]
    left_all = [left_half, core_swap(left_half)]
    group = jnp.stack([shared[:16], partner[:16]])
    group = after(group, *left_all, *right)
    group = jnp.stack([group, across(group)])

    contact, weights = outer(
        seqs, residues, left_all, right, contact_matrix, product_weight, mixing_logit_matrix[0].T
    )
    group = after(group, weights)
    behind, ahead = along_y(group, 1), along_y(group, 3)
    weights = route(weights, lambda z, x, y, h, c: (y, 2 * h + c, z, x >> 1, x & 1))
    pair = transition(contact, feedforward_gate_expand[0], feedforward_shrink_matrix[0])
    weights, behind, ahead, pair = lax.optimization_barrier((weights, behind, ahead, pair))
    weights = jnp.stack([weights[0]] + [along_z(weights[v & 1], v) for v in (1, 2, 3)])
    opposite = jnp.stack([along_y(behind[0], 1), along_y(ahead[1], 3)])
    weights, opposite = lax.optimization_barrier((weights, opposite))
    after_x, before_x = along_x(weights, 1), along_x(weights, 3)
    weights = [weights, after_x, along_x(after_x[:2], 1), along_x(before_x[2:], 3), before_x]
    everyone = jnp.stack([group, behind, opposite, ahead])
    everyone = [everyone, core_swap(everyone)]
    own, other = average(weights, everyone, value_weight, gate_weight, mixing_weight)
    msa = epilogue([own, along_z(other, 1)], homolog)
    return jnp.swapaxes(msa, 1, 2), pair


def solution(mesh):
    split = jax.sharding.PartitionSpec("row", "col", None)
    whole = jax.sharding.PartitionSpec()
    return jax.shard_map(
        local, mesh=mesh, in_specs=(split, split) + (whole,) * 9, out_specs=(split, split), check_vma=False
    )
```

```python
import jax
import jax.numpy as jnp
from jax import lax
from jax.experimental import pallas as pl
from jax.experimental.pallas import tpu as pltpu

F32 = jnp.float32
BF = jnp.bfloat16
ROWS = 16


def normalize(field, axis=-1):
    center = field - jnp.mean(field, axis=axis, keepdims=True)
    spread = jnp.mean(center * center, axis=axis, keepdims=True)
    return center * lax.rsqrt(spread + 1e-5)


def full(shape):
    return pl.BlockSpec(shape, lambda *_: (0,) * len(shape))


def wide(value, lanes):
    missing = jnp.zeros((*value.shape[:-1], lanes - value.shape[-1]), value.dtype)
    return jnp.concatenate([value, missing], axis=-1)


def tall(value, rows):
    missing = jnp.zeros((rows - value.shape[0], *value.shape[1:]), value.dtype)
    return jnp.concatenate([value, missing], axis=0)


def call(body, scalars, grid, in_specs, out_specs, out_shape, scratch, cost, limit=48):
    flops, moved, special = cost
    return pl.pallas_call(
        body,
        grid_spec=pltpu.PrefetchScalarGridSpec(
            num_scalar_prefetch=scalars, grid=grid, in_specs=in_specs, out_specs=out_specs, scratch_shapes=scratch
        ),
        out_shape=out_shape,
        compiler_params=pltpu.CompilerParams(vmem_limit_bytes=limit * 1024 * 1024),
        cost_estimate=pl.CostEstimate(flops=flops, bytes_accessed=moved, transcendentals=special),
        name=body.__name__,
    )


def shaped(dtype, *dims):
    return jax.ShapeDtypeStruct(dims, dtype)


def prologue_body(seqs, residues, homolog, weight, left_out, right_out, shared_out, left_rows, right_rows):
    row, col = lax.axis_index("row"), lax.axis_index("col")
    normed = normalize(homolog[...].astype(F32), 1)
    rounded = normed.astype(BF)
    weights = weight[...].astype(F32)
    left_weight = jnp.concatenate([weights[:, :32]] * 4, axis=1).astype(BF)
    right_weight = jnp.transpose(wide(weights, 128))[32:64].astype(BF)
    for s in range(8):
        right_rows[s] = wide(jnp.dot(right_weight, rounded[s], preferred_element_type=F32), 128)
    turned = jnp.transpose(wide(normed.reshape(512, 80), 128))[:80].astype(BF)
    for k in range(5):
        shared_out[:16, k * 512 : (k + 1) * 512] = turned[k * 16 : (k + 1) * 16]
    for s in range(8):
        left_rows[s] = jnp.dot(turned[:, s * 64 : (s + 1) * 64], left_weight, preferred_element_type=F32)
    lane = lax.broadcasted_iota(jnp.int32, (8, 128), 1)
    seq_ok = row * 8 + lax.broadcasted_iota(jnp.int32, (8, 128), 0) < seqs[0]
    group = lane // 32
    for q in range(20):
        piece = left_rows[:, 4 * q, :]
        for k in range(1, 4):
            piece = jnp.where(group == k, left_rows[:, 4 * q + k, :], piece)
        ok = seq_ok & (col * 80 + 4 * q + group < residues[0])
        left_out[:, q * 128 : (q + 1) * 128] = jnp.where(ok, piece, 0.0).astype(BF)
    ok = seq_ok & (col * 80 + lane < residues[0])
    pieces = [jnp.where(ok, right_rows[:, d, :], 0.0)[:, :80] for d in range(32)]
    pieces = jnp.concatenate(pieces, axis=1).astype(BF)
    right_out[...] = pieces
    shared_out[16:, :] = pieces


def prologue(seqs, residues, homolog, weight):
    return call(
        prologue_body, 2, (1,),
        [full((8, 64, 80)), full((64, 64))],
        [full((8, 2560)), full((8, 2560)), full((24, 2560))],
        [shaped(BF, 8, 2560), shaped(BF, 8, 2560), shaped(BF, 24, 2560)],
        [pltpu.VMEM((8, 80, 128), F32), pltpu.VMEM((8, 32, 128), F32)],
        (10**8, 4 * 10**5, 10**4),
    )(seqs, residues, homolog, weight)


def weights_body(product, value_gate, mixing, product_out, value_out, gate_out, mixing_out, rows):
    rows[...] = product[...].astype(F32).reshape(32, 32, 128)
    swapped = jnp.concatenate([rows[:, d, :] for d in range(32)], axis=0)
    product_out[...] = jnp.transpose(swapped).astype(BF)
    value_out[...] = jnp.zeros_like(value_out)
    gate_out[...] = jnp.zeros_like(gate_out)
    mixing_out[...] = jnp.zeros_like(mixing_out)
    both = value_gate[...]
    final = jnp.transpose(tall(mixing[...].astype(F32), 128))[:, :64].astype(BF)
    for h in range(8):
        for s in range(4):
            value_out[h, s * 64 : (s + 1) * 64, s * 32 : (s + 1) * 32] = both[:, h * 32 : (h + 1) * 32]
            gate_out[h, s * 64 : (s + 1) * 64, s * 32 : (s + 1) * 32] = both[:, 256 + h * 32 : 288 + h * 32]
            mixing_out[h, s * 32 : (s + 1) * 32, s * 64 : (s + 1) * 64] = final[h * 32 : (h + 1) * 32]


def arrange_weights(product, value_gate, mixing):
    return call(
        weights_body, 0, (1,),
        [full((1024, 128)), full((64, 512)), full((64, 256))],
        [full((128, 1024)), full((8, 256, 128)), full((8, 256, 128)), full((8, 128, 256))],
        [shaped(BF, 128, 1024), shaped(BF, 8, 256, 128), shaped(BF, 8, 256, 128), shaped(BF, 8, 128, 256)],
        [pltpu.VMEM((32, 32, 128), F32)],
        (10**6, 2 * 10**6, 0),
    )(product, value_gate, mixing)


def outer_body(seqs, residues, left_a, left_b, right_a, right_b, right_c, right_d, contact, final_weight, logit_weight,
               contact_out, weights_out, left_t, right_p, products, expo, flat):
    step = pl.program_id(0)
    row, col = lax.axis_index("row"), lax.axis_index("col")

    @pl.when(step == 0)
    def _():
        for w, half in enumerate((left_a, left_b)):
            for v in range(4):
                for u in range(2):
                    flat[(w * 8 + v * 2 + u) * 8 : (w * 8 + v * 2 + u + 1) * 8, :] = half[v, u].astype(F32)
        left_t[...] = jnp.transpose(flat[...]).astype(BF)
        for m, part in enumerate((right_a, right_b, right_c, right_d)):
            for v in range(4):
                z = (row >> 2) ^ v
                x = (row - m) & 3
                place = ((col ^ x) & 1) * 8 + (((col >> 2) - z) & 3) * 2 + (((col >> 1) ^ (x >> 1)) & 1)
                flat[pl.ds(pl.multiple_of(place * 8, 8), 8), :] = part[v].astype(F32)
        rows = flat[...]
        for d in range(32):
            right_p[:, d * 128 : (d + 1) * 128] = wide(rows[:, d * 80 : (d + 1) * 80], 128).astype(BF)

    inverse = 1.0 / seqs[0].astype(F32)
    lane = lax.broadcasted_iota(jnp.int32, (8 * ROWS, 128), 1)
    rows = left_t[pl.ds(pl.multiple_of(step * 32 * ROWS, 32 * ROWS), 32 * ROWS), :]
    for n in range(8):
        product = jnp.dot(rows, right_p[:, n * 512 : (n + 1) * 512], preferred_element_type=F32)
        product = (product * inverse).astype(BF)
        for i in range(ROWS):
            for q in range(4):
                d = n * 4 + q
                products[d * 32 : (d + 1) * 32, i * 128 : (i + 1) * 128] = product[
                    i * 32 : (i + 1) * 32, q * 128 : (q + 1) * 128
                ]
    updates = []
    for i in range(0, ROWS, 2):
        update = jnp.dot(final_weight[...], products[:, i * 128 : (i + 2) * 128], preferred_element_type=F32)
        updates += [jnp.transpose(update[:, :128])[:80], jnp.transpose(update[:, 128:])[:80]]
    fresh = contact[...].reshape(ROWS * 80, 128).astype(F32) + jnp.concatenate(updates, axis=0)
    fresh = fresh.astype(BF)
    contact_out[...] = fresh.reshape(ROWS, 80, 128)
    normed = normalize(fresh.astype(F32)).astype(BF)
    logits = jnp.concatenate(
        [
            lax.dot_general(
                logit_weight[...], tall(normed[i * 80 : (i + 1) * 80], 128), (((1,), (1,)), ((), ())),
                preferred_element_type=F32,
            )
            for i in range(ROWS)
        ],
        axis=0,
    )
    logits = jnp.where(col * 80 + lane < residues[0], logits, -1e9)
    peak = jnp.max(jnp.where(lane < 80, logits, -3e38), axis=-1, keepdims=True)
    terms = jnp.where(lane < 80, jnp.exp(logits - peak), 0.0)
    total = jnp.sum(terms, axis=-1, keepdims=True)
    for k, value in enumerate((peak, total)):
        high = value.astype(BF).astype(F32)
        middle = (value - high).astype(BF).astype(F32)
        for t, part in enumerate((high, middle, value - high - middle)):
            terms = jnp.where(lane == 80 + 3 * k + t, part, terms)
    expo[pl.ds(step * ROWS, ROWS)] = terms.reshape(ROWS, 8, 128)

    @pl.when(step == 80 // ROWS - 1)
    def _():
        for q in range(2):
            weights_out[q] = expo[pl.ds((((col >> 2) + q) & 1) * 40, 40)].reshape(320, 128).astype(BF)


def outer(seqs, residues, left, right, contact, final_weight, logit_weight):
    block = pl.BlockSpec((ROWS, 80, 128), lambda g, *_: (g, 0, 0))
    return call(
        outer_body, 2, (80 // ROWS,),
        [full((4, 2, 8, 2560))] * 2 + [full((4, 8, 2560))] * 4 + [block, full((128, 1024)), full((8, 128))],
        [block, full((2, 320, 128))],
        [shaped(BF, 80, 80, 128), shaped(BF, 2, 320, 128)],
        [
            pltpu.VMEM((2560, 128), BF), pltpu.VMEM((128, 4096), BF), pltpu.VMEM((1024, 128 * ROWS), BF),
            pltpu.VMEM((80, 8, 128), F32), pltpu.VMEM((128, 2560), F32),
        ],
        (12 * 10**9, 6 * 10**6, 10**5),
    )(seqs, residues, *left, *right, contact, final_weight, logit_weight)


def transition_body(contact, up_weight, down_weight, out):
    rows = contact[...].reshape(640, 128).astype(F32)
    normed = normalize(rows).astype(BF)
    hidden = jnp.dot(normed, up_weight[...], preferred_element_type=F32)
    gate = hidden[:, :512]
    active = (gate * jax.nn.sigmoid(gate) * hidden[:, 512:]).astype(BF)
    rows = rows + jnp.dot(active, down_weight[...], preferred_element_type=F32)
    out[...] = rows.astype(BF).reshape(8, 80, 128)


def transition(contact, up_weight, down_weight):
    block = pl.BlockSpec((8, 80, 128), lambda g: (g, 0, 0))
    return call(
        transition_body, 0, (10,),
        [block, full((128, 1024)), full((512, 128))],
        block, shaped(BF, 80, 80, 128), [],
        (5 * 10**9, 33 * 10**5, 6400 * 512), 32,
    )(contact, up_weight, down_weight)


def average_body(part_a, part_b, part_c, part_d, part_e, everyone_a, everyone_b, value_weight, gate_weight, final_weight,
                 out_a, out_b, scaled, mixed, normed):
    row, col = lax.axis_index("row"), lax.axis_index("col")
    parts = (part_a, part_b, (part_c.at[0], part_c.at[1], part_d.at[0], part_d.at[1]), part_e)
    blocks = [(x, z) for x in range(4) for z in range(4)]
    lane = lax.broadcasted_iota(jnp.int32, (320, 128), 1)

    def block(x, z):
        return (parts[x][z][...] if x == 2 else parts[x][z]).astype(F32)

    def stat(x, z, k):
        here = (lane >= 80 + 3 * k) & (lane < 83 + 3 * k)
        return jnp.sum(jnp.where(here, block(x, z), 0.0), axis=-1, keepdims=True)

    peaks = [stat(x, z, 0) for x, z in blocks]
    peak = peaks[0]
    for other in peaks[1:]:
        peak = jnp.maximum(peak, other)
    factors = [jnp.exp(p - peak) for p in peaks]
    total = sum(f * stat(x, z, 1) for f, (x, z) in zip(factors, blocks))
    inverse = 1.0 / total
    for factor, (x, z) in zip(factors, blocks):
        far_z = (row >> 2) ^ z
        far_x = (row - x) & 3
        place = ((col ^ far_x) & 1) * 8 + (((col >> 2) - far_z) & 3) * 2 + (((col >> 1) ^ (far_x >> 1)) & 1)
        scaled[place] = block(x, z) * (factor * inverse)
    for w, everyone in enumerate((everyone_a, everyone_b)):
        for v in range(4):
            for u in range(2):
                for k in range(5):
                    start = (w * 8 + v * 2 + u) * 80 + k * 16
                    for z in range(2):
                        normed[start : start + 16, z * 512 : (z + 1) * 512] = everyone[v, u, z, :, k * 512 : (k + 1) * 512]
    sums = None
    for w in range(2):
        rows = jnp.concatenate([scaled[w * 8 + k][:, :80] for k in range(8)], axis=1).astype(BF)
        term = jnp.dot(rows, normed[w * 640 : (w + 1) * 640, :], preferred_element_type=F32)
        sums = term if sums is None else sums + term
    mixed[...] = sums.reshape(40, 8, 1024)
    pick = lax.broadcasted_iota(jnp.int32, (40, 80), 1) - ((row >> 2) & 1) * 40
    pick = pick == lax.broadcasted_iota(jnp.int32, (40, 80), 0)
    own = jnp.dot(pick.astype(F32).astype(BF), normed[:80, :], preferred_element_type=F32)

    def stacked(value):
        return jnp.concatenate([value[:, g * 256 : (g + 1) * 256] for g in range(4)], axis=0).astype(BF)

    own = stacked(own)
    result = None
    for h in range(8):
        value = jnp.dot(stacked(mixed[:, h, :]), value_weight[h], preferred_element_type=F32)
        gate = jnp.dot(own, gate_weight[h], preferred_element_type=F32)
        gated = (jax.nn.sigmoid(gate) * value).astype(BF)
        term = jnp.dot(gated, final_weight[h], preferred_element_type=F32)
        result = term if result is None else result + term
    out_a[...] = result[:80]
    out_b[...] = result[80:]


def average(parts, everyone, value_weight, gate_weight, final_weight):
    return call(
        average_body, 0, (1,),
        [full((4, 320, 128))] * 2 + [full((2, 320, 128))] * 2 + [full((4, 320, 128))] + [full((4, 2, 2, 16, 2560))] * 2 + [
            full((8, 256, 128)), full((8, 256, 128)), full((8, 128, 256))
        ],
        [full((80, 256))] * 2, [shaped(F32, 80, 256)] * 2,
        [pltpu.VMEM((16, 320, 128), F32), pltpu.VMEM((40, 8, 1024), F32), pltpu.VMEM((1280, 1024), BF)],
        (3 * 10**9, 8 * 10**6, 10**5), 36,
    )(*parts, *everyone, value_weight, gate_weight, final_weight)


def epilogue_body(part_a, part_b, homolog, out, pieces):
    parity = (lax.axis_index("row") >> 2) & 1
    pieces[0] = part_a[...]
    pieces[1] = part_b[...]
    for half in range(2):
        rows = jnp.concatenate([pieces[parity ^ q][half * 40 : half * 40 + 40] for q in range(2)], axis=0)
        turned = jnp.transpose(tall(rows, 128))
        for s in range(4):
            fresh = homolog[half * 4 + s].astype(F32) + turned[s * 64 : (s + 1) * 64, :80]
            out[half * 4 + s] = fresh.astype(BF)


def epilogue(parts, homolog):
    return call(
        epilogue_body, 0, (1,),
        [full((80, 256))] * 2 + [full((8, 64, 80))], full((8, 64, 80)), shaped(BF, 8, 64, 80),
        [pltpu.VMEM((2, 80, 256), F32)],
        (10**6, 4 * 10**5, 0),
    )(*parts, homolog)


def place(z, x, y, h, core):
    return (z * 4 + x) * 16 + y * 4 + h * 2 + core


def route(value, target):
    pairs = []
    for index in range(256):
        row, col = divmod(index, 16)
        z, x, y, h, core = row >> 2, row & 3, col >> 2, (col >> 1) & 1, col & 1
        pairs.append((index, place(*target(z, x, y, h, core))))
    return lax.ppermute(value, ("row", "col"), pairs)


def along_x(value, m):
    return route(value, lambda z, x, y, h, c: (z, (x + m) % 4, y, h, c))


def along_z(value, m):
    return route(value, lambda z, x, y, h, c: (z ^ m, x, y, h, c))


def along_y(value, m):
    return route(value, lambda z, x, y, h, c: (z, x, (y + m) % 4, h, c))


ALONG = {
    "x": ("row", [[4 * z + x for x in range(4)] for z in range(4)]),
    "z": ("row", [[4 * z + x for z in range(4)] for x in range(4)]),
    "y": ("col", [[4 * y + j for y in range(4)] for j in range(4)]),
}


def exchange(values, line):
    axis, groups = ALONG[line]
    return lax.all_to_all(values, axis, 0, 0, axis_index_groups=groups, tiled=True)


def from_line(value, line):
    return exchange(jnp.broadcast_to(value[None], (4, *value.shape)), line)


def across(value):
    return route(value, lambda z, x, y, h, c: (z, x, y, h ^ 1, c))


def core_swap(value):
    return route(value, lambda z, x, y, h, c: (z, x, y, h, c ^ 1))


def after(value, *others):
    return lax.optimization_barrier((value, *others))[0]


def local(
    homolog_matrix,
    contact_matrix,
    seqs,
    residues,
    tensor_product_matrices,
    tensor_product_final,
    mixing_value_gate_matrix,
    mixing_logit_matrix,
    mixing_final_matrix,
    feedforward_gate_expand,
    feedforward_shrink_matrix,
):
    homolog = jnp.swapaxes(homolog_matrix, 1, 2)
    left, right, shared = prologue(seqs, residues, homolog, tensor_product_matrices[0])

    halves = jnp.stack([
        route(left, lambda z, x, y, h, c, u=u: (y, 2 * h + c, z, (x >> 1) ^ u, x & 1)) for u in range(2)
    ])
    partner = along_z(shared, 1)
    column = jnp.stack([right, partner[16:]] + [along_z(right, m) for m in (2, 3)])
    left_half = jnp.stack([halves] + [along_y(halves, m) for m in (1, 2, 3)])
    right = [column] + [along_x(column, m) for m in (1, 3, 2)]
    right[2], right[3] = right[3], right[2]
    left_all = [left_half, core_swap(left_half)]
    product_weight, value_weight, gate_weight, mixing_weight = arrange_weights(
        after(tensor_product_final[0], left_half), mixing_value_gate_matrix[0], mixing_final_matrix[0].T
    )
    group = jnp.stack([shared[:16], partner[:16]])
    group = after(group, right[3])
    group = jnp.stack([group, across(group)])

    contact, weights = outer(
        seqs, residues, left_all, right, contact_matrix, product_weight, mixing_logit_matrix[0].T
    )
    group = after(group, weights)
    behind, ahead = along_y(group, 1), along_y(group, 3)
    weights = route(weights, lambda z, x, y, h, c: (y, 2 * h + c, z, x >> 1, x & 1))
    pair = transition(contact, feedforward_gate_expand[0], feedforward_shrink_matrix[0])
    weights, behind, ahead, pair = lax.optimization_barrier((weights, behind, ahead, pair))
    weights = jnp.stack([weights[0]] + [along_z(weights[v & 1], v) for v in (1, 2, 3)])
    opposite = jnp.stack([along_y(behind[0], 1), along_y(ahead[1], 3)])
    weights, opposite = lax.optimization_barrier((weights, opposite))
    after_x, before_x = along_x(weights, 1), along_x(weights, 3)
    weights = [weights, after_x, along_x(after_x[:2], 1), along_x(before_x[2:], 3), before_x]
    everyone = jnp.stack([group, behind, opposite, ahead])
    everyone = [everyone, core_swap(everyone)]
    own, other = average(weights, everyone, value_weight, gate_weight, mixing_weight)
    msa = epilogue([own, along_z(other, 1)], homolog)
    return jnp.swapaxes(msa, 1, 2), pair


def solution(mesh):
    split = jax.sharding.PartitionSpec("row", "col", None)
    whole = jax.sharding.PartitionSpec()
    return jax.shard_map(
        local, mesh=mesh, in_specs=(split, split) + (whole,) * 9, out_specs=(split, split), check_vma=False
    )
```
